128 devices in a mesh: section: 4 (over x), seq: 16 (over z, y), dp: 2 (over core).
Axes of the slice: x: 4, y: 4, z: 4, core: 2. Of those that a mesh axis runs over, the one named last changes fastest.
Arguments:
- video_query: bfloat16 [4, 2, 2048, 2048], P('section', 'dp', 'seq'), may hold values from -40 to 40
- video_value: bfloat16 [4, 2, 2048, 2048], P('section', 'dp', 'seq'), may hold values from -6 to 6
- video_cot: bfloat16 [4, 2, 2048, 2048], P('section', 'dp', 'seq'), may hold values from -6 to 6
- text_key: bfloat16 [4, 2, 2048, 2048], P('section', 'dp', 'seq'), may hold values from -6 to 6
- text_value: bfloat16 [4, 2, 2048, 2048], P('section', 'dp', 'seq'), may hold values from -6 to 6
- text_cot: bfloat16 [4, 2, 2048, 2048], P('section', 'dp', 'seq'), may hold values from -6 to 6
- pair_blocks: int32 [4, 2, 16, 4], P('section', 'dp', 'seq'), may hold values from -1 to 15, as said below
- pair_count: int32 [4, 2, 16], P('section', 'dp', 'seq'), may hold values from 1 to 4, as said below
- learned_logit_multiplier: float32 [4, 16], P('section'), may hold values from 0.5 to 2
Outputs:
- video_out: bfloat16 [4, 2, 2048, 2048], P('section', 'dp', 'seq')
- text_out: bfloat16 [4, 2, 2048, 2048], P('section', 'dp', 'seq')
- video_query_grad: bfloat16 [4, 2, 2048, 2048], P('section', 'dp', 'seq')
- video_value_grad: bfloat16 [4, 2, 2048, 2048], P('section', 'dp', 'seq')
- text_key_grad: bfloat16 [4, 2, 2048, 2048], P('section', 'dp', 'seq')
- text_value_grad: bfloat16 [4, 2, 2048, 2048], P('section', 'dp', 'seq')
- scale_grad: float32 [4, 16], P('section')
The draws below stay inside these ranges and needn't reach their ends.
Inputs may be any that keep to these rules, and one draw needn't show every extreme that they name: `pair_blocks`: the listed entries of a row are distinct text blocks; entries past pair_count are -1; every text block of a micro-batch is listed in some row. `pair_count`: in every micro-batch some video block has 4 pairs and some has one.
All inputs are finite; a program needn't handle non-finite values.
Results may differ from the reference program's by a relative error of at most 0.017.
The reference program's roundings to bfloat16 on the way count: a program that leaves them out, or rounds other values in their place, can miss the bound.
Values may be sent and summed in bfloat16 or wider, within the bound.
A program may use at most 256 MiB of HBM per device.

```python
import math
import jax
import jax.numpy as jnp
from jax import lax

HEADS = 16
HEAD_SIZE = 128
HD = 2048
BLK = 128
VB_DEV = 1
PMAX = 4
NTB = 16
NVB = 16
NT = 2048
NV = 2048
N_SECTION = 4
N_SEQ = 16
N_DP = 2


def query_key(key):
    base = jax.random.fold_in(key, 7)
    first, second = jax.random.split(base, 2)
    query_shape = (N_SECTION, N_DP, NV, HD)
    key_shape = (N_SECTION, N_DP, NT, HD)
    queries = jnp.clip(jax.random.normal(first, query_shape, jnp.float32), -6.0, 6.0)
    keys = jnp.clip(jax.random.normal(second, key_shape, jnp.float32), -6.0, 6.0)
    return (queries, keys)


def draw_video_query(key, part):
    return query_key(key)[0].astype(jnp.bfloat16)


def draw_text_key(key, part):
    return query_key(key)[1].astype(jnp.bfloat16)


def pair_lists(key):
    base = jax.random.fold_in(key, 31)
    first, second, third, fourth = jax.random.split(base, 4)
    groups = N_SECTION * N_DP
    heavy = jax.random.randint(first, (groups, NVB), 0, 4) == 0
    light = jax.random.randint(second, (groups, NVB), 1, 3)
    coupling_tallies = jnp.where(heavy, PMAX, light)
    full_at = jax.random.randint(third, (groups, 1), 0, NVB)
    block_pos = jnp.arange(NVB)[None, :]
    coupling_tallies = jnp.where(block_pos == full_at, PMAX, coupling_tallies)
    coupling_tallies = jnp.where(block_pos == (full_at + 1) % NVB, 1, coupling_tallies)
    draws = jax.random.randint(fourth, (groups, NVB, NTB - 1), 0, 2 ** 20) * NTB + jnp.arange(NTB - 1)
    order = jnp.argsort(draws, axis=-1, stable=True).astype(jnp.int32)
    offsets = jnp.concatenate([jnp.zeros((groups, NVB, 1), jnp.int32), order[:, :, :PMAX - 1] + 1], axis=-1)
    home = (jnp.arange(NVB) * NTB // NVB)[None, :, None]
    enumerated_couplings = (home + offsets) % NTB
    enumerated_couplings = jnp.where(jnp.arange(PMAX)[None, None, :] < coupling_tallies[:, :, None], enumerated_couplings, -1)
    return (enumerated_couplings.reshape(N_SECTION, N_DP, NVB, PMAX).astype(jnp.int32), coupling_tallies.reshape(N_SECTION, N_DP, NVB).astype(jnp.int32))


def draw_pair_blocks(key, part):
    return pair_lists(key)[0]


def draw_pair_count(key, part):
    return pair_lists(key)[1]


def levels(stream_key, shape, cuts, least, high):
    gain, own = 1.0, jax.random.fold_in(stream_key, 6)
    for axis_at, shards_of in cuts:
        steps = jnp.exp(jax.random.uniform(jax.random.fold_in(own, axis_at), (shards_of,), jnp.float32, least / len(cuts), high / len(cuts)))
        gain = gain * jnp.repeat(steps, shape[axis_at] // shards_of).reshape([-1 if axis == axis_at else 1 for axis in range(len(shape))])
    return gain


def centred(key, dims, width, most, cuts=(), dtype=jnp.bfloat16):
    loudness = levels(key, dims, cuts, -0.22, 0.18) if cuts else 1.0
    values = jax.random.normal(key, dims, jnp.float32) * width * loudness
    return jnp.minimum(jnp.maximum(values, -most), most).astype(dtype)


def setup_inputs(seed: int = 0) -> dict:
    key_of = jax.random.split(jax.random.key(seed), 10)
    return {
        "video_query": draw_video_query(jax.random.fold_in(key_of[9], 71), 0),
        "video_value": centred(key_of[1], (N_SECTION, N_DP, NV, HD), 1.0, 6.0, ((0, 4), (1, 2), (2, 16))),
        "video_cot": centred(key_of[2], (N_SECTION, N_DP, NV, HD), 1.0, 6.0, ((0, 4), (1, 2), (2, 16))),
        "text_key": draw_text_key(jax.random.fold_in(key_of[9], 71), 0),
        "text_value": centred(key_of[4], (N_SECTION, N_DP, NT, HD), 1.0, 6.0, ((0, 4), (1, 2), (2, 16))),
        "text_cot": centred(key_of[5], (N_SECTION, N_DP, NT, HD), 1.0, 6.0, ((0, 4), (1, 2), (2, 16))),
        "pair_blocks": draw_pair_blocks(jax.random.fold_in(key_of[9], 71), 0),
        "pair_count": draw_pair_count(jax.random.fold_in(key_of[9], 71), 0),
        "learned_logit_multiplier": jnp.clip(jnp.exp(math.log(2.0) - 1.3862944 * jax.random.uniform(key_of[8], (N_SECTION, HEADS), jnp.float32) ** levels(key_of[8], (N_SECTION, HEADS), ((0, 4),), -0.2, 0.2)), 0.5, 2.0),
    }


NEG_FILL = -1.0e30


def block_mask(enumerated_couplings, coupling_tallies):
    slot_pos = jnp.arange(enumerated_couplings.shape[1])
    live = slot_pos[None, :] < coupling_tallies[:, None]
    block_ids = jnp.arange(N_SEQ)
    hits = (enumerated_couplings[:, :, None] == block_ids[None, None, :]) & live[:, :, None]
    return jnp.any(hits, axis=1)


def attend_one_channel(clip_probe_channelwise, caption_lookup_channelwise, caption_payload_channelwise, clip_payload_channelwise, clip_adjoint_channelwise, caption_adjoint_channelwise, sharpness_multiplier, entire_admission_grid):
    scale_factor = HEAD_SIZE ** -0.5
    unnormalized_logits = jnp.dot(clip_probe_channelwise, caption_lookup_channelwise.T, preferred_element_type=jnp.float32) * scale_factor
    affinity_logits = sharpness_multiplier * unnormalized_logits
    masked = jnp.where(entire_admission_grid, affinity_logits, NEG_FILL)
    row_max = jnp.max(masked, axis=1, keepdims=True)
    row_exp = jnp.where(entire_admission_grid, jnp.exp(affinity_logits - row_max), 0.0)
    row_prob = row_exp / jnp.sum(row_exp, axis=1, keepdims=True)
    row_half = row_prob.astype(jnp.bfloat16)
    video_f = jnp.dot(row_half, caption_payload_channelwise, preferred_element_type=jnp.float32)
    col_max = jnp.max(masked, axis=0, keepdims=True)
    col_exp = jnp.where(entire_admission_grid, jnp.exp(affinity_logits - col_max), 0.0)
    col_sum = jnp.sum(col_exp, axis=0, keepdims=True)
    rows_per_device = VB_DEV * BLK
    column_group_list = col_exp.astype(jnp.bfloat16).astype(jnp.float32).reshape(N_SEQ, rows_per_device, -1)
    video_value_groups = clip_payload_channelwise.astype(jnp.float32).reshape(N_SEQ, rows_per_device, HEAD_SIZE)
    text_fragments = jnp.einsum("csl,csm->clm", column_group_list, video_value_groups, precision=lax.Precision.HIGHEST)
    text_fragments = lax.optimization_barrier(text_fragments.astype(jnp.bfloat16))
    text_f = jnp.sum(text_fragments.astype(jnp.float32), axis=0) / col_sum.T
    column_dot_grad = jnp.dot(clip_payload_channelwise, caption_adjoint_channelwise.T, preferred_element_type=jnp.float32)
    col_delta = jnp.sum(col_exp * column_dot_grad, axis=0, keepdims=True) / col_sum
    col_prob = col_exp / col_sum
    row_dp = jnp.dot(clip_adjoint_channelwise, caption_payload_channelwise.T, preferred_element_type=jnp.float32)
    row_delta = jnp.sum(clip_adjoint_channelwise.astype(jnp.float32) * video_f, axis=1, keepdims=True)
    derivative_logits = row_prob * (row_dp - row_delta) + col_prob * (column_dot_grad - col_delta)
    scale_term = jnp.sum(derivative_logits * unnormalized_logits)
    derivative_share = (sharpness_multiplier * derivative_logits).astype(jnp.bfloat16)
    query_grad = jnp.dot(derivative_share, caption_lookup_channelwise, preferred_element_type=jnp.float32) * scale_factor
    value_grad = jnp.dot(col_prob.astype(jnp.bfloat16), caption_adjoint_channelwise, preferred_element_type=jnp.float32)
    gradient_group_list = derivative_share.astype(jnp.float32).reshape(N_SEQ, rows_per_device, -1)
    query_group_list = clip_probe_channelwise.astype(jnp.float32).reshape(N_SEQ, rows_per_device, HEAD_SIZE)
    halved_groups = row_half.astype(jnp.float32).reshape(N_SEQ, rows_per_device, -1)
    cotangent_group_list = clip_adjoint_channelwise.astype(jnp.float32).reshape(N_SEQ, rows_per_device, HEAD_SIZE)
    key_fragments = jnp.einsum("csl,csm->clm", gradient_group_list, query_group_list, precision=lax.Precision.HIGHEST) * scale_factor
    text_value_fragments = jnp.einsum("csl,csm->clm", halved_groups, cotangent_group_list, precision=lax.Precision.HIGHEST)
    key_fragments = lax.optimization_barrier(key_fragments.astype(jnp.bfloat16))
    text_value_fragments = lax.optimization_barrier(text_value_fragments.astype(jnp.bfloat16))
    key_grad = jnp.sum(key_fragments.astype(jnp.float32), axis=0)
    tval_grad = jnp.sum(text_value_fragments.astype(jnp.float32), axis=0)
    return (video_f.astype(jnp.bfloat16), text_f.astype(jnp.bfloat16), query_grad.astype(jnp.bfloat16),
            value_grad.astype(jnp.bfloat16), key_grad.astype(jnp.bfloat16), tval_grad.astype(jnp.bfloat16), scale_term)


def split_into_channels(values):
    return values.reshape(values.shape[0], HEADS, HEAD_SIZE).transpose(1, 0, 2)


def join_heads(values):
    return values.transpose(1, 0, 2).reshape(values.shape[1], HEADS * HEAD_SIZE)


def subset_sample_tally(clip_probe_subset, clip_payload_subset, clip_adjoint_subset, caption_lookup_subset, caption_payload_subset, caption_adjoint_subset, enumerated_couplings, coupling_tallies, sharpness_multiplier_line):
    small_mask = block_mask(enumerated_couplings, coupling_tallies)
    entire_admission_grid = jnp.repeat(jnp.repeat(small_mask, BLK, axis=0), BLK, axis=1)

    def run_head(pieces):
        return attend_one_channel(pieces[0], pieces[1], pieces[2], pieces[3], pieces[4], pieces[5], pieces[6], entire_admission_grid)

    results = lax.map(run_head, (split_into_channels(clip_probe_subset), split_into_channels(caption_lookup_subset), split_into_channels(caption_payload_subset),
                                 split_into_channels(clip_payload_subset), split_into_channels(clip_adjoint_subset), split_into_channels(caption_adjoint_subset), sharpness_multiplier_line))
    return (join_heads(results[0]), join_heads(results[1]), join_heads(results[2]), join_heads(results[3]),
            join_heads(results[4]), join_heads(results[5]), results[6])


def reference(video_query, video_value, video_cot, text_key, text_value, text_cot, pair_blocks, pair_count, learned_logit_multiplier):
    groups = N_SECTION * N_DP

    def flatten(values):
        return values.reshape((groups,) + values.shape[2:])

    tempers = jnp.repeat(learned_logit_multiplier, N_DP, axis=0)

    def run_batch(pieces):
        return subset_sample_tally(*pieces)

    results = lax.map(run_batch, (flatten(video_query), flatten(video_value), flatten(video_cot), flatten(text_key),
                                  flatten(text_value), flatten(text_cot), flatten(pair_blocks), flatten(pair_count), tempers))

    def unflatten(values):
        return values.reshape((N_SECTION, N_DP) + values.shape[1:])

    video_out = unflatten(results[0])
    text_out = unflatten(results[1])
    scale_grad = jnp.sum(unflatten(results[6]), axis=1)
    query_grad = jnp.roll(unflatten(results[2]), -1, axis=0)
    value_grad = jnp.roll(unflatten(results[3]), -1, axis=0)
    key_grad = jnp.roll(unflatten(results[4]), -1, axis=0)
    tval_grad = jnp.roll(unflatten(results[5]), -1, axis=0)
    return (video_out, text_out, query_grad, value_grad, key_grad, tval_grad, scale_grad)
```

```python
import functools

import jax
import jax.numpy as jnp
from jax import lax
from jax.experimental import pallas as pl
from jax.experimental.pallas import tpu as pltpu
from jax.sharding import PartitionSpec as P

MESH = pl.DeviceIdType.MESH
NEG_FILL = -1e30
F32 = jnp.float32
BF16 = jnp.bfloat16
NT_DIMS = (((1,), (1,)), ((), ()))
TN_DIMS = (((0,), (0,)), ((), ()))


def spread_kernel(n_seq, d, *refs):
    srcs, pair_src = refs[:6], refs[6]
    dsts, pair_dst = refs[7:13], refs[13]
    send_sem, recv_sem, pair_send, pair_recv, own_sem, pair_own = refs[14:]
    me = lax.axis_index("seq")

    def peer_of(k):
        return lax.rem(me + k, n_seq)

    barrier = pltpu.get_barrier_semaphore()

    @pl.loop(1, n_seq)
    def _(k):
        pl.semaphore_signal(barrier, inc=1, device_id={"seq": peer_of(k)}, device_id_type=MESH)

    pl.semaphore_wait(barrier, n_seq - 1)

    def pair_copy(k):
        return pltpu.make_async_remote_copy(
            src_ref=pair_src,
            dst_ref=pair_dst.at[me],
            send_sem=pair_send.at[k],
            recv_sem=pair_recv.at[k],
            device_id={"seq": peer_of(k)},
            device_id_type=MESH,
        )

    def copy(a, k):
        peer = peer_of(k)
        return pltpu.make_async_remote_copy(
            src_ref=srcs[a].at[:, pl.ds(pl.multiple_of(peer * d, d), d)],
            dst_ref=dsts[a].at[me],
            send_sem=send_sem.at[a, k],
            recv_sem=recv_sem.at[a, k],
            device_id={"seq": peer},
            device_id_type=MESH,
        )

    def own(a):
        return pltpu.make_async_copy(
            srcs[a].at[:, pl.ds(pl.multiple_of(me * d, d), d)], dsts[a].at[me], own_sem.at[a]
        )

    own_pair = pltpu.make_async_copy(pair_src, pair_dst.at[me], pair_own)
    own_pair.start()

    @pl.loop(1, n_seq)
    def _(k):
        pair_copy(k).start()

    for a in range(6):

        @pl.loop(1, n_seq)
        def _(k):
            copy(a, k).start()

        own(a).start()

    own_pair.wait()

    @pl.loop(1, n_seq)
    def _(k):
        pair_copy(k).wait()

    for a in range(6):
        own(a).wait()

        @pl.loop(1, n_seq)
        def _(k):
            copy(a, k).wait()


def attend_kernel(
    n_blk,
    scale,
    pair_ref,
    mult_ref,
    q_ref,
    vv_ref,
    vc_ref,
    k_ref,
    tv_ref,
    tc_ref,
    video_out,
    text_out,
    q_grad,
    v_grad,
    k_grad,
    t_grad,
    scale_out,
    score_buf,
    grad_buf,
    exp_buf,
    dot_buf,
    k_sel,
    tv_sel,
    tc_sel,
    text_acc,
    key_acc,
    tval_acc,
    col_max,
    col_sum,
    col_dot,
    scale_acc,
):
    head = lax.axis_index("seq")
    mult = mult_ref[0, head]
    blk = q_ref.shape[1]

    def nt(x, y):
        return lax.dot_general(x, y, NT_DIMS, preferred_element_type=F32)

    def tn(x, y):
        return lax.dot_general(x, y, TN_DIMS, preferred_element_type=F32)

    def nn(x, y):
        return jnp.dot(x, y, preferred_element_type=F32)

    def half(x):
        return x.astype(BF16).astype(F32)

    text_acc[...] = jnp.zeros_like(text_acc)
    key_acc[...] = jnp.zeros_like(key_acc)
    tval_acc[...] = jnp.zeros_like(tval_acc)
    col_max[...] = jnp.full_like(col_max, NEG_FILL)
    col_sum[...] = jnp.zeros_like(col_sum)
    col_dot[...] = jnp.zeros_like(col_dot)
    scale_acc[...] = jnp.zeros_like(scale_acc)

    def slots(i, width):
        picks = [pair_ref[i, 0, p] for p in range(width)]
        return picks, [jnp.maximum(x, 0) for x in picks]

    def pick(width, index, pairs):
        for source, held in pairs:
            for p in range(width):
                held[p * blk : (p + 1) * blk, :] = source[index[p]]

    def cut(x, p):
        return x[:, p * blk : (p + 1) * blk]

    def rows_first(i, width):
        picks, index = slots(i, width)
        wide = width * blk
        pick(width, index, ((k_ref, k_sel), (tv_ref, tv_sel)))
        query, cot = q_ref[i], vc_ref[i]
        score = nt(query, k_sel[:wide]) * (mult * scale)
        score = jnp.concatenate(
            [
                jnp.where(picks[p] >= 0, cut(score, p), NEG_FILL) if p else cut(score, 0)
                for p in range(width)
            ],
            axis=1,
        )
        score_buf[i, :, :wide] = score
        top = jnp.max(score, axis=0, keepdims=True)
        for p in range(width):
            at = pl.ds(index[p], 1)
            col_max[at, :] = jnp.maximum(col_max[at, :], cut(top, p))
        row_exp = jnp.exp(score - jnp.max(score, axis=1, keepdims=True))
        row_prob = row_exp / jnp.sum(row_exp, axis=1, keepdims=True)
        row_half = row_prob.astype(BF16)
        video_f = nn(row_half, tv_sel[:wide])
        video_out[i] = video_f.astype(BF16)
        row_dp = nt(cot, tv_sel[:wide])
        row_delta = jnp.sum(cot.astype(F32) * video_f, axis=1, keepdims=True)
        grad_buf[i, :, :wide] = row_prob * (row_dp - row_delta)
        piece = tn(row_half, cot)
        for p in range(width):
            tval_acc[index[p]] += half(piece[p * blk : (p + 1) * blk])

    def columns(i, width):
        _, index = slots(i, width)
        wide = width * blk
        pick(width, index, ((tc_ref, tc_sel),))
        value = vv_ref[i]
        tops = jnp.concatenate([col_max[pl.ds(index[p], 1), :] for p in range(width)], axis=1)
        col_exp = jnp.exp(score_buf[i, :, :wide] - tops)
        col_dp = nt(value, tc_sel[:wide])
        exp_buf[i, :, :wide] = col_exp
        dot_buf[i, :, :wide] = col_dp
        total = jnp.sum(col_exp, axis=0, keepdims=True)
        dots = jnp.sum(col_exp * col_dp, axis=0, keepdims=True)
        piece = tn(col_exp.astype(BF16), value)
        for p in range(width):
            at = pl.ds(index[p], 1)
            col_sum[at, :] += cut(total, p)
            col_dot[at, :] += cut(dots, p)
            text_acc[index[p]] += half(piece[p * blk : (p + 1) * blk])

    def rows_last(i, width):
        _, index = slots(i, width)
        wide = width * blk
        pick(width, index, ((k_ref, k_sel), (tc_ref, tc_sel)))
        sums = jnp.concatenate([col_max[pl.ds(index[p], 1), :] for p in range(width)], axis=1)
        delta = jnp.concatenate([col_dot[pl.ds(index[p], 1), :] for p in range(width)], axis=1)
        col_prob = exp_buf[i, :, :wide] * sums
        grad = grad_buf[i, :, :wide] + col_prob * (dot_buf[i, :, :wide] - delta)
        tally = jnp.sum(grad * score_buf[i, :, :wide], axis=0, keepdims=True)
        for p in range(width):
            scale_acc[...] += cut(tally, p)
        grad_half = (mult * grad).astype(BF16)
        q_grad[i] = (nn(grad_half, k_sel[:wide]) * scale).astype(BF16)
        v_grad[i] = nn(col_prob.astype(BF16), tc_sel[:wide]).astype(BF16)
        piece = tn(grad_half, q_ref[i]) * scale
        for p in range(width):
            key_acc[index[p]] += half(piece[p * blk : (p + 1) * blk])

    def over_blocks(work):
        @pl.loop(0, n_blk)
        def _(i):
            few = pair_ref[i, 0, 2] < 0

            @pl.when(few)
            def _():
                work(i, 2)

            @pl.when(jnp.logical_not(few))
            def _():
                work(i, 4)

    over_blocks(rows_first)
    over_blocks(columns)
    inverse = 1.0 / col_sum[...]
    col_max[...] = inverse
    col_dot[...] = col_dot[...] * inverse
    turned = jnp.transpose(inverse)
    for j in range(n_blk):
        text_out[j] = (text_acc[j] * turned[:, j : j + 1]).astype(BF16)
    over_blocks(rows_last)
    k_grad[...] = key_acc[...].astype(BF16)
    t_grad[...] = tval_acc[...].astype(BF16)
    total = jnp.sum(scale_acc[...], axis=1, keepdims=True) / mult
    scale_out[...] = jnp.broadcast_to(total, scale_out.shape)


def collect_kernel(n_seq, n_section, d, *refs):
    srcs, scale_src = refs[:6], refs[6]
    dsts, scale_dst = refs[7:13], refs[13]
    send_sem, recv_sem, scale_send, scale_recv, own_sem, scale_own = refs[14:]
    me, section, core = lax.axis_index("seq"), lax.axis_index("section"), lax.axis_index("dp")
    before = lax.rem(section + n_section - 1, n_section)
    after = lax.rem(section + 1, n_section)

    def peer_of(k):
        return lax.rem(me + k, n_seq)

    barrier = pltpu.get_barrier_semaphore()

    @pl.loop(0, n_seq)
    def _(k):
        pl.semaphore_signal(
            barrier, inc=1, device_id={"seq": peer_of(k), "section": after}, device_id_type=MESH
        )
        pl.semaphore_signal(
            barrier, inc=1, device_id={"seq": peer_of(k), "dp": 1 - core}, device_id_type=MESH
        )

    @pl.loop(1, n_seq)
    def _(k):
        pl.semaphore_signal(barrier, inc=1, device_id={"seq": peer_of(k)}, device_id_type=MESH)

    pl.semaphore_wait(barrier, 3 * n_seq - 1)

    def scale_copy(k, other):
        return pltpu.make_async_remote_copy(
            src_ref=scale_src,
            dst_ref=scale_dst.at[core, me],
            send_sem=scale_send.at[other, k],
            recv_sem=scale_recv.at[other, k],
            device_id={"seq": peer_of(k), "dp": (1 - core) if other else core},
            device_id_type=MESH,
        )

    def copy(a, k):
        peer = peer_of(k)
        where = {"seq": peer} if a < 2 else {"seq": peer, "section": before}
        return pltpu.make_async_remote_copy(
            src_ref=srcs[a].at[peer],
            dst_ref=dsts[a].at[:, pl.ds(pl.multiple_of(me * d, d), d)],
            send_sem=send_sem.at[a, k],
            recv_sem=recv_sem.at[a, k],
            device_id=where,
            device_id_type=MESH,
        )

    def own(a):
        return pltpu.make_async_copy(
            srcs[a].at[me], dsts[a].at[:, pl.ds(pl.multiple_of(me * d, d), d)], own_sem.at[a]
        )

    own_scale = pltpu.make_async_copy(scale_src, scale_dst.at[core, me], scale_own)
    own_scale.start()

    @pl.loop(0, n_seq)
    def _(k):
        scale_copy(k, 1).start()

    @pl.loop(1, n_seq)
    def _(k):
        scale_copy(k, 0).start()

    for a in (2, 3, 4, 5, 0, 1):

        @pl.loop(1 if a < 2 else 0, n_seq)
        def _(k):
            copy(a, k).start()

        if a < 2:
            own(a).start()

    own_scale.wait()

    @pl.loop(0, n_seq)
    def _(k):
        scale_copy(k, 1).wait()

    @pl.loop(1, n_seq)
    def _(k):
        scale_copy(k, 0).wait()

    for a in (2, 3, 4, 5, 0, 1):

        @pl.loop(1 if a < 2 else 0, n_seq)
        def _(k):
            copy(a, k).wait()

        if a < 2:
            own(a).wait()


def on_device(n_seq, n_section, *arrays):
    rows, pair_blocks, multiplier = arrays[:6], arrays[6], arrays[8]
    blk, width = rows[0].shape[2:]
    heads = multiplier.shape[1]
    d = width // heads
    slots = pair_blocks.shape[3]
    anywhere = pl.BlockSpec(memory_space=pl.ANY)
    vmem = pl.BlockSpec(memory_space=pltpu.VMEM)
    smem = pl.BlockSpec(memory_space=pltpu.SMEM)
    cube = jax.ShapeDtypeStruct((n_seq, blk, d), BF16)
    flat = jax.ShapeDtypeStruct((blk, width), BF16)

    spread = pl.pallas_call(
        functools.partial(spread_kernel, n_seq, d),
        out_shape=(cube,) * 6 + (jax.ShapeDtypeStruct((n_seq, 1, slots), jnp.int32),),
        in_specs=[anywhere] * 7,
        out_specs=(anywhere,) * 7,
        scratch_shapes=[
            pltpu.SemaphoreType.DMA((6, n_seq)),
            pltpu.SemaphoreType.DMA((6, n_seq)),
            pltpu.SemaphoreType.DMA((n_seq,)),
            pltpu.SemaphoreType.DMA((n_seq,)),
            pltpu.SemaphoreType.DMA((6,)),
            pltpu.SemaphoreType.DMA,
        ],
        compiler_params=pltpu.CompilerParams(collective_id=0, has_side_effects=True),
        name="spread",
    )(*[x[0, 0] for x in rows], pair_blocks[0, 0])
    query, value, cot, key, tval, tcot, pairs = spread

    wide = slots * blk
    results = pl.pallas_call(
        functools.partial(attend_kernel, n_seq, d ** (-0.5)),
        out_shape=(cube,) * 6 + (jax.ShapeDtypeStruct((8, 128), F32),),
        in_specs=[smem, smem] + [vmem] * 6,
        out_specs=(vmem,) * 7,
        scratch_shapes=[pltpu.VMEM((n_seq, blk, wide), F32)] * 4
        + [pltpu.VMEM((wide, d), BF16)] * 3
        + [pltpu.VMEM((n_seq, blk, d), F32)] * 3
        + [pltpu.VMEM((n_seq, blk), F32)] * 3
        + [pltpu.VMEM((1, blk), F32)],
        compiler_params=pltpu.CompilerParams(vmem_limit_bytes=48 * 1024 * 1024),
        name="attend",
    )(pairs, multiplier, query, value, cot, key, tval, tcot)

    collected = pl.pallas_call(
        functools.partial(collect_kernel, n_seq, n_section, d),
        out_shape=(flat,) * 6 + (jax.ShapeDtypeStruct((2, n_seq, 8, 128), F32),),
        in_specs=[anywhere] * 7,
        out_specs=(anywhere,) * 7,
        scratch_shapes=[
            pltpu.SemaphoreType.DMA((6, n_seq)),
            pltpu.SemaphoreType.DMA((6, n_seq)),
            pltpu.SemaphoreType.DMA((2, n_seq)),
            pltpu.SemaphoreType.DMA((2, n_seq)),
            pltpu.SemaphoreType.DMA((6,)),
            pltpu.SemaphoreType.DMA,
        ],
        compiler_params=pltpu.CompilerParams(collective_id=1, has_side_effects=True),
        name="collect",
    )(*results)
    scale_total = jnp.sum(collected[6][:, :, 0, 0], axis=0)
    return tuple(x[None, None] for x in collected[:6]) + (scale_total[None],)


def solution(mesh):
    main = P("section", "dp", "seq", None)
    in_specs = (main,) * 7 + (P("section", "dp", "seq"), P("section", None))
    out_specs = (main,) * 6 + (P("section", None),)
    body = functools.partial(on_device, mesh.shape["seq"], mesh.shape["section"])
    return jax.shard_map(body, mesh=mesh, in_specs=in_specs, out_specs=out_specs, check_vma=False)
```

```python
import functools

import jax
import jax.numpy as jnp
from jax import lax
from jax.experimental import pallas as pl
from jax.experimental.pallas import tpu as pltpu
from jax.sharding import PartitionSpec as P

MESH = pl.DeviceIdType.MESH
NEG_FILL = -1e30
F32 = jnp.float32
BF16 = jnp.bfloat16
NT_DIMS = (((1,), (1,)), ((), ()))
TN_DIMS = (((0,), (0,)), ((), ()))
QUERY, VALUE, COT, KEY, TVAL, TCOT = range(6)
VIDEO_OUT, TEXT_OUT, QUERY_GRAD, VALUE_GRAD, KEY_GRAD, TVAL_GRAD = range(6)
ARRIVAL = (KEY, QUERY, TCOT, VALUE, TVAL, COT)


def fused_kernel(n_seq, n_section, slots, scale, *refs):
    srcs, pair_src, mult_src = refs[:6], refs[6], refs[7]
    outs, scale_all, pair_all = refs[8:14], refs[14], refs[15]
    land, results, scale_own = refs[16:22], refs[22:28], refs[28]
    score_buf, row_buf, col_buf, dot_buf = refs[29:33]
    k_sel, t_sel, c_sel = refs[33:36]
    text_acc, key_acc, tval_acc = refs[36:39]
    top_acc, sum_acc, dot_acc, scale_acc = refs[39:43]
    pairs, newest, prior, final = refs[43:47]
    (in_send, in_recv, in_own, out_send, out_recv, out_own, pair_send, pair_recv, pair_own) = refs[47:56]
    scale_send, scale_recv, scale_sem, mult_ref, mult_sem = refs[56:]

    me, section, core = lax.axis_index("seq"), lax.axis_index("section"), lax.axis_index("dp")
    before = lax.rem(section + n_section - 1, n_section)
    after = lax.rem(section + 1, n_section)
    blk, d = land[0].shape[1:]
    wide = slots * blk
    empty = n_seq * slots
    mine = pl.ds(pl.multiple_of(me * d, d), d)

    def turn(k):
        return lax.rem(me + k, n_seq)

    def nt(x, y):
        return lax.dot_general(x, y, NT_DIMS, preferred_element_type=F32)

    def tn(x, y):
        return lax.dot_general(x, y, TN_DIMS, preferred_element_type=F32)

    def nn(x, y):
        return jnp.dot(x, y, preferred_element_type=F32)

    def half(x):
        return x.astype(BF16).astype(F32)

    def remote(src, dst, send, recv, **where):
        return pltpu.make_async_remote_copy(
            src_ref=src, dst_ref=dst, send_sem=send, recv_sem=recv, device_id=where, device_id_type=MESH
        )

    def inbound(a, k):
        peer = turn(k)
        piece = srcs[a].at[:, pl.ds(pl.multiple_of(peer * d, d), d)]
        return remote(piece, land[a].at[me], in_send.at[a, k], in_recv.at[a, k], seq=peer)

    def inbound_own(a):
        return pltpu.make_async_copy(srcs[a].at[:, mine], land[a].at[me], in_own.at[a])

    def pair_copy(k):
        return remote(pair_src, pair_all.at[me], pair_send.at[k], pair_recv.at[k], seq=turn(k))

    def outbound(a, k):
        peer = turn(k)
        ends = (results[a].at[peer], outs[a].at[:, mine], out_send.at[a, k], out_recv.at[a, k])
        if a in (VIDEO_OUT, TEXT_OUT):
            return remote(*ends, seq=peer)
        return remote(*ends, seq=peer, section=before)

    def outbound_own(a):
        return pltpu.make_async_copy(results[a].at[me], outs[a].at[:, mine], out_own.at[a])

    def send_out(a, k):
        if a in (VIDEO_OUT, TEXT_OUT):

            @pl.when(k == 0)
            def _():
                outbound_own(a).start()

            @pl.when(k > 0)
            def _():
                outbound(a, k).start()

        else:
            outbound(a, k).start()

    def scale_copy(other, k):
        return remote(
            scale_own,
            scale_all.at[core, me],
            scale_send.at[other, k],
            scale_recv.at[other, k],
            seq=turn(k),
            dp=(1 - core) if other else core,
        )

    barrier = pltpu.get_barrier_semaphore()

    @pl.loop(1, n_seq)
    def _(k):
        pl.semaphore_signal(barrier, inc=1, device_id={"seq": turn(k)}, device_id_type=MESH)

    @pl.loop(0, n_seq)
    def _(k):
        pl.semaphore_signal(
            barrier, inc=1, device_id={"seq": turn(k), "section": after}, device_id_type=MESH
        )
        pl.semaphore_signal(
            barrier, inc=1, device_id={"seq": turn(k), "dp": 1 - core}, device_id_type=MESH
        )

    pl.semaphore_wait(barrier, 3 * n_seq - 1)

    own_pairs = pltpu.make_async_copy(pair_src, pair_all.at[me], pair_own)
    own_pairs.start()

    @pl.loop(1, n_seq)
    def _(k):
        pair_copy(k).start()

    for a in ARRIVAL:

        @pl.loop(1, n_seq)
        def _(k):
            inbound(a, k).start()

        inbound_own(a).start()

    fetch_mult = pltpu.make_async_copy(mult_src, mult_ref, mult_sem)
    fetch_mult.start()
    own_pairs.wait()

    @pl.loop(1, n_seq)
    def _(k):
        pair_copy(k).wait()

    fetch_mult.wait()
    mult = mult_ref[0, me]

    listed = pltpu.make_async_copy(pair_all, pairs, pair_own)
    listed.start()
    text_acc[empty] = jnp.zeros((blk, d), F32)
    key_acc[empty] = jnp.zeros((blk, d), F32)
    tval_acc[empty] = jnp.zeros((blk, d), F32)
    top_acc[empty] = jnp.full((1, blk), NEG_FILL, F32)
    sum_acc[empty] = jnp.zeros((1, blk), F32)
    dot_acc[empty] = jnp.zeros((1, blk), F32)
    scale_acc[...] = jnp.zeros_like(scale_acc)
    listed.wait()

    for j in range(n_seq):
        newest[j] = empty

    @pl.loop(0, n_seq)
    def _(k):
        i = turn(k)
        for p in range(slots):
            j = pairs[i, 0, p]
            slot = i * slots + p
            prior[slot] = jnp.where(j >= 0, newest[jnp.maximum(j, 0)], empty)
            for b in range(n_seq):
                newest[b] = jnp.where(j == b, slot, newest[b])

    @pl.loop(0, n_seq)
    def _(i):
        for p in range(slots):
            final[i * slots + p] = newest[jnp.maximum(pairs[i, 0, p], 0)]

    def arrive(*arrays):
        for a in arrays:
            inbound_own(a).wait()

            @pl.loop(1, n_seq)
            def _(k):
                inbound(a, k).wait()

    def cut(x, p):
        return x[:, p * blk : (p + 1) * blk]

    def pick(i, source, held):
        for p in range(slots):
            held[p * blk : (p + 1) * blk, :] = source[jnp.maximum(pairs[i, 0, p], 0)]

    def spread_out(i, rows):
        return jnp.concatenate([rows[final[i * slots + p]] for p in range(slots)], axis=1)

    def chain(i, acc, join, parts):
        for p in range(slots):
            slot = i * slots + p
            acc[slot] = join(acc[prior[slot]], parts[p])

    def add(x, y):
        return x + y

    def blocks(piece):
        return [half(piece[p * blk : (p + 1) * blk]) for p in range(slots)]

    arrive(KEY, QUERY)

    @pl.loop(0, n_seq)
    def _(k):
        i = turn(k)
        pick(i, land[KEY], k_sel)
        score = nt(land[QUERY][i], k_sel[...]) * (mult * scale)
        score = jnp.concatenate(
            [
                jnp.where(pairs[i, 0, p] >= 0, cut(score, p), NEG_FILL)
                for p in range(slots)
            ],
            axis=1,
        )
        score_buf[i] = score
        top = jnp.max(score, axis=0, keepdims=True)
        chain(i, top_acc, jnp.maximum, [cut(top, p) for p in range(slots)])
        row_exp = jnp.exp(score - jnp.max(score, axis=1, keepdims=True))
        row_buf[i] = row_exp / jnp.sum(row_exp, axis=1, keepdims=True)

    @pl.loop(0, n_seq)
    def _(k):
        i = turn(k)
        col_exp = jnp.exp(score_buf[i] - spread_out(i, top_acc))
        col_buf[i] = col_exp
        total = jnp.sum(col_exp, axis=0, keepdims=True)
        chain(i, sum_acc, add, [cut(total, p) for p in range(slots)])

    sum_acc[...] = 1.0 / sum_acc[...]

    arrive(TCOT, VALUE)

    @pl.loop(0, n_seq)
    def _(k):
        i = turn(k)
        pick(i, land[TCOT], c_sel)
        value = land[VALUE][i]
        col_exp = col_buf[i]
        col_prob = col_exp * spread_out(i, sum_acc)
        results[VALUE_GRAD][i] = nn(col_prob.astype(BF16), c_sel[...]).astype(BF16)
        send_out(VALUE_GRAD, k)
        col_dp = nt(value, c_sel[...])
        dots = jnp.sum(col_exp * col_dp, axis=0, keepdims=True)
        chain(i, dot_acc, add, [cut(dots, p) for p in range(slots)])
        chain(i, text_acc, add, blocks(tn(col_exp.astype(BF16), value)))
        col_buf[i] = col_prob
        dot_buf[i] = col_dp

    dot_acc[...] = dot_acc[...] * sum_acc[...]

    @pl.loop(0, n_seq)
    def _(k):
        j = turn(k)
        at = newest[j]
        weight = jnp.transpose(jnp.broadcast_to(sum_acc[at], (blk, blk)))
        results[TEXT_OUT][j] = (text_acc[at] * weight).astype(BF16)
        send_out(TEXT_OUT, k)

    arrive(TVAL, COT)

    @pl.loop(0, n_seq)
    def _(k):
        i = turn(k)
        pick(i, land[KEY], k_sel)
        pick(i, land[TVAL], t_sel)
        cot = land[COT][i]
        row_prob = row_buf[i]
        row_half = row_prob.astype(BF16)
        video_f = nn(row_half, t_sel[...])
        results[VIDEO_OUT][i] = video_f.astype(BF16)
        send_out(VIDEO_OUT, k)
        row_dp = nt(cot, t_sel[...])
        row_delta = jnp.sum(cot.astype(F32) * video_f, axis=1, keepdims=True)
        grad = row_prob * (row_dp - row_delta) + col_buf[i] * (dot_buf[i] - spread_out(i, dot_acc))
        tally = jnp.sum(grad * score_buf[i], axis=0, keepdims=True)
        for p in range(slots):
            scale_acc[...] += cut(tally, p)
        grad_half = (mult * grad).astype(BF16)
        results[QUERY_GRAD][i] = (nn(grad_half, k_sel[...]) * scale).astype(BF16)
        send_out(QUERY_GRAD, k)
        chain(i, key_acc, add, blocks(tn(grad_half, land[QUERY][i]) * scale))
        chain(i, tval_acc, add, blocks(tn(row_half, cot)))

    total = jnp.sum(scale_acc[...], axis=1, keepdims=True) / mult
    scale_own[...] = jnp.broadcast_to(total, scale_own.shape)

    @pl.loop(0, n_seq)
    def _(k):
        j = turn(k)
        at = newest[j]
        results[KEY_GRAD][j] = key_acc[at].astype(BF16)
        send_out(KEY_GRAD, k)
        results[TVAL_GRAD][j] = tval_acc[at].astype(BF16)
        send_out(TVAL_GRAD, k)

    own_scale = pltpu.make_async_copy(scale_own, scale_all.at[core, me], scale_sem)
    own_scale.start()

    @pl.loop(1, n_seq)
    def _(k):
        scale_copy(0, k).start()

    @pl.loop(0, n_seq)
    def _(k):
        scale_copy(1, k).start()

    own_scale.wait()

    @pl.loop(1, n_seq)
    def _(k):
        scale_copy(0, k).wait()

    @pl.loop(0, n_seq)
    def _(k):
        scale_copy(1, k).wait()

    for a in range(6):
        if a in (VIDEO_OUT, TEXT_OUT):
            outbound_own(a).wait()

        @pl.loop(1 if a in (VIDEO_OUT, TEXT_OUT) else 0, n_seq)
        def _(k):
            outbound(a, k).wait()


def deliver_kernel(n_seq, *refs):
    srcs, scale_all, dsts, scale_out, sems = refs[:6], refs[6], refs[7:13], refs[13], refs[14]
    copies = [pltpu.make_async_copy(s, t, sems.at[a]) for a, (s, t) in enumerate(zip(srcs, dsts))]
    for c in copies:
        c.start()
    lane = lax.broadcasted_iota(jnp.int32, (8, 128), 1)
    total = jnp.zeros((8, 128), F32)
    for h in range(n_seq):
        total = jnp.where(lane == h, scale_all[0, h] + scale_all[1, h], total)
    scale_out[...] = total[:1, :n_seq]
    for c in copies:
        c.wait()


def on_device(n_seq, n_section, *arrays):
    rows, pair_blocks, multiplier = arrays[:6], arrays[6], arrays[8]
    blk, width = rows[0].shape[2:]
    d = width // multiplier.shape[1]
    slots = pair_blocks.shape[3]
    vmem = pl.BlockSpec(memory_space=pltpu.VMEM)
    hbm = pl.BlockSpec(memory_space=pltpu.HBM)
    flat = jax.ShapeDtypeStruct((blk, width), BF16)
    places = n_seq * slots + 1
    dma = pltpu.SemaphoreType.DMA

    fused = pl.pallas_call(
        functools.partial(fused_kernel, n_seq, n_section, slots, d ** (-0.5)),
        out_shape=(flat,) * 6
        + (
            jax.ShapeDtypeStruct((2, n_seq, 8, 128), F32),
            jax.ShapeDtypeStruct((n_seq, 1, slots), jnp.int32),
        ),
        in_specs=[hbm] * 8,
        out_specs=(vmem,) * 7 + (hbm,),
        scratch_shapes=[pltpu.VMEM((n_seq, blk, d), BF16)] * 12
        + [pltpu.VMEM((8, 128), F32)]
        + [pltpu.VMEM((n_seq, blk, slots * blk), F32)] * 4
        + [pltpu.VMEM((slots * blk, d), BF16)] * 3
        + [pltpu.VMEM((places, blk, d), F32)] * 3
        + [pltpu.VMEM((places, 1, blk), F32)] * 3
        + [pltpu.VMEM((1, blk), F32)]
        + [
            pltpu.SMEM((n_seq, 1, slots), jnp.int32),
            pltpu.SMEM((n_seq,), jnp.int32),
            pltpu.SMEM((places,), jnp.int32),
            pltpu.SMEM((places,), jnp.int32),
        ]
        + [dma((6, n_seq)), dma((6, n_seq)), dma((6,))] * 2
        + [dma((n_seq,)), dma((n_seq,)), dma]
        + [dma((2, n_seq)), dma((2, n_seq)), dma]
        + [pltpu.SMEM(multiplier.shape, F32), dma],
        compiler_params=pltpu.CompilerParams(
            collective_id=0, has_side_effects=True, vmem_limit_bytes=101 * 512 * 1024
        ),
        name="fused",
    )(*[x[0, 0] for x in rows], pair_blocks[0, 0], multiplier)

    delivered = pl.pallas_call(
        functools.partial(deliver_kernel, n_seq),
        out_shape=(flat,) * 6 + (jax.ShapeDtypeStruct((1, n_seq), F32),),
        in_specs=[vmem] * 7,
        out_specs=(hbm,) * 6 + (vmem,),
        scratch_shapes=[dma((6,))],
        compiler_params=pltpu.CompilerParams(vmem_limit_bytes=2 * 1024 * 1024),
        name="deliver",
    )(*fused[:7])
    return tuple(x[None, None] for x in delivered[:6]) + (delivered[6],)


def solution(mesh):
    main = P("section", "dp", "seq", None)
    in_specs = (main,) * 7 + (P("section", "dp", "seq"), P("section", None))
    out_specs = (main,) * 6 + (P("section", None),)
    body = functools.partial(on_device, mesh.shape["seq"], mesh.shape["section"])
    return jax.shard_map(body, mesh=mesh, in_specs=in_specs, out_specs=out_specs, check_vma=False)
```

```python
import functools

import jax
import jax.numpy as jnp
from jax import lax
from jax.experimental import pallas as pl
from jax.experimental.pallas import tpu as pltpu
from jax.sharding import PartitionSpec as P

MESH = pl.DeviceIdType.MESH
NEG_FILL = -1e30
F32 = jnp.float32
BF16 = jnp.bfloat16
NT_DIMS = (((1,), (1,)), ((), ()))
TN_DIMS = (((0,), (0,)), ((), ()))
QUERY, VALUE, COT, KEY, TVAL, TCOT = range(6)
VIDEO_OUT, TEXT_OUT, QUERY_GRAD, VALUE_GRAD, KEY_GRAD, TVAL_GRAD = range(6)
ARRIVAL = (KEY, QUERY, VALUE, TVAL, TCOT, COT)


def fused_kernel(n_seq, n_section, slots, scale, *refs):
    srcs, pair_src, mult_src = refs[:6], refs[6], refs[7]
    outs, scale_out, pair_all = refs[8:14], refs[14], refs[15]
    land, results, scale_own = refs[16:22], refs[22:28], refs[28]
    score_buf, row_buf, col_buf, dot_buf = refs[29:33]
    k_sel, t_sel, c_sel = refs[33:36]
    text_acc, key_acc, tval_acc = refs[36:39]
    top_acc, sum_acc, dot_acc, scale_acc = refs[39:43]
    pairs, newest, prior, final = refs[43:47]
    (in_send, in_recv, in_own, out_send, out_recv, out_own, pair_send, pair_recv, pair_own) = refs[47:56]
    scale_send, scale_recv, mult_send, mult_recv, own_sem = refs[56:61]
    scale_land, mult_land, mult_ref, video_buf = refs[61:]

    me, section, core = lax.axis_index("seq"), lax.axis_index("section"), lax.axis_index("dp")
    before = lax.rem(section + n_section - 1, n_section)
    after = lax.rem(section + 1, n_section)
    worker = lax.rem(section + n_section - core, n_section)
    home = lax.rem(section + core, n_section)
    previous = lax.rem(section + core + n_section - 1, n_section)
    blk, d = land[0].shape[1:]
    wide = slots * blk
    empty = n_seq * slots
    mine = pl.ds(pl.multiple_of(me * d, d), d)

    def turn(k):
        return lax.rem(me + k, n_seq)

    def back(k):
        return lax.rem(me + n_seq - k, n_seq)

    def nt(x, y):
        return lax.dot_general(x, y, NT_DIMS, preferred_element_type=F32)

    def tn(x, y):
        return lax.dot_general(x, y, TN_DIMS, preferred_element_type=F32)

    def nn(x, y):
        return jnp.dot(x, y, preferred_element_type=F32)

    def half(x):
        return x.astype(BF16).astype(F32)

    def remote(src, dst, send, recv, **where):
        return pltpu.make_async_remote_copy(
            src_ref=src, dst_ref=dst, send_sem=send, recv_sem=recv, device_id=where, device_id_type=MESH
        )

    def inbound(a, k):
        peer = turn(k)
        piece = srcs[a].at[:, pl.ds(pl.multiple_of(peer * d, d), d)]
        return remote(
            piece, land[a].at[me], in_send.at[a, k], in_recv.at[a, k], seq=peer, section=worker
        )

    def inbound_own(a):
        return pltpu.make_async_copy(srcs[a].at[:, mine], land[a].at[me], in_own.at[a])

    def pair_copy(k):
        return remote(
            pair_src, pair_all.at[me], pair_send.at[k], pair_recv.at[k], seq=turn(k), section=worker
        )

    def pair_copy_own():
        return pltpu.make_async_copy(pair_src, pair_all.at[me], pair_own)

    def outbound(a, k):
        peer = back(k)
        ends = (results[a].at[peer], outs[a].at[:, mine], out_send.at[a, k], out_recv.at[a, k])
        where = home if a in (VIDEO_OUT, TEXT_OUT) else previous
        return remote(*ends, seq=peer, section=where)

    def outbound_own(a):
        return pltpu.make_async_copy(results[a].at[me], outs[a].at[:, mine], out_own.at[a])

    def either(is_own, own, other):
        pl.when(is_own)(own)
        pl.when(jnp.logical_not(is_own))(other)

    def stays(a, k):
        return k + (core if a in (VIDEO_OUT, TEXT_OUT) else 1 - core) == 0

    def send_out(a, k):
        either(stays(a, k), lambda: outbound_own(a).start(), lambda: outbound(a, k).start())

    def send_all(*kinds):
        for a in kinds:

            @pl.loop(0, n_seq)
            def _(k):
                send_out(a, k)

    def scale_copy(other, k):
        return remote(
            scale_own,
            scale_land.at[core, me],
            scale_send.at[other, k],
            scale_recv.at[other, k],
            seq=turn(k),
            section=home,
            dp=(1 - core) if other else core,
        )

    def scale_copy_own():
        return pltpu.make_async_copy(scale_own, scale_land.at[core, me], own_sem)

    def mult_copy():
        return remote(mult_src, mult_land, mult_send, mult_recv, section=worker)

    def mult_copy_own():
        return pltpu.make_async_copy(mult_src, mult_land, own_sem)

    barrier = pltpu.get_barrier_semaphore()

    @pl.loop(1, n_seq)
    def _(k):
        pl.semaphore_signal(barrier, inc=1, device_id={"seq": turn(k)}, device_id_type=MESH)

    def signal_all(where, to):
        @pl.loop(0, n_seq)
        def _(k):
            there = {"seq": turn(k), "section": where, "dp": to}
            pl.semaphore_signal(barrier, inc=1, device_id=there, device_id_type=MESH)

    signal_all(after, core)

    @pl.when(core == 0)
    def _():
        signal_all(before, 1)
        pl.semaphore_wait(barrier, 3 * n_seq - 1)

    @pl.when(core == 1)
    def _():
        signal_all(before, 1)
        signal_all(section, 0)
        pl.semaphore_wait(barrier, 4 * n_seq - 1)

    @pl.loop(0, n_seq)
    def _(k):
        either(k + core == 0, lambda: pair_copy_own().start(), lambda: pair_copy(k).start())

    either(core == 0, lambda: mult_copy_own().start(), lambda: mult_copy().start())
    for a in ARRIVAL:

        @pl.loop(0, n_seq)
        def _(k):
            either(k + core == 0, lambda: inbound_own(a).start(), lambda: inbound(a, k).start())

    @pl.loop(0, n_seq)
    def _(k):
        either(k + core == 0, lambda: pair_copy_own().wait(), lambda: pair_copy(k).wait())

    either(core == 0, lambda: mult_copy_own().wait(), lambda: mult_copy().wait())
    fetch_mult = pltpu.make_async_copy(mult_land, mult_ref, own_sem)
    fetch_mult.start()
    fetch_mult.wait()
    mult = mult_ref[0, me]

    listed = pltpu.make_async_copy(pair_all, pairs, pair_own)
    listed.start()
    text_acc[empty] = jnp.zeros((blk, d), F32)
    key_acc[empty] = jnp.zeros((blk, d), F32)
    tval_acc[empty] = jnp.zeros((blk, d), F32)
    top_acc[empty] = jnp.full((1, blk), NEG_FILL, F32)
    sum_acc[empty] = jnp.zeros((1, blk), F32)
    dot_acc[empty] = jnp.zeros((1, blk), F32)
    scale_acc[...] = jnp.zeros_like(scale_acc)
    listed.wait()

    for j in range(n_seq):
        newest[j] = empty

    @pl.loop(0, n_seq)
    def _(k):
        i = back(k)
        for p in range(slots):
            j = pairs[i, 0, p]
            slot = i * slots + p
            prior[slot] = jnp.where(j >= 0, newest[jnp.maximum(j, 0)], empty)
            for b in range(n_seq):
                newest[b] = jnp.where(j == b, slot, newest[b])

    @pl.loop(0, n_seq)
    def _(i):
        for p in range(slots):
            final[i * slots + p] = newest[jnp.maximum(pairs[i, 0, p], 0)]

    def arrive_one(a, k):
        either(k + core == 0, lambda: inbound_own(a).wait(), lambda: inbound(a, k).wait())

    def arrive(a):
        @pl.loop(0, n_seq)
        def _(k):
            arrive_one(a, k)

    def cut(x, p):
        return x[:, p * blk : (p + 1) * blk]

    def pick(i, source, held):
        for p in range(slots):
            held[p * blk : (p + 1) * blk, :] = source[jnp.maximum(pairs[i, 0, p], 0)]

    def spread_out(i, rows):
        return jnp.concatenate([rows[final[i * slots + p]] for p in range(slots)], axis=1)

    def chain(i, acc, join, parts):
        for p in range(slots):
            slot = i * slots + p
            acc[slot] = join(acc[prior[slot]], parts[p])

    def add(x, y):
        return x + y

    def blocks(piece):
        return [half(piece[p * blk : (p + 1) * blk]) for p in range(slots)]

    arrive(KEY)

    @pl.loop(0, n_seq)
    def _(k):
        i = back(k)
        arrive_one(QUERY, k)
        pick(i, land[KEY], k_sel)
        score = nt(land[QUERY][i], k_sel[...]) * (mult * scale)
        score = jnp.concatenate(
            [
                jnp.where(pairs[i, 0, p] >= 0, cut(score, p), NEG_FILL)
                for p in range(slots)
            ],
            axis=1,
        )
        score_buf[i] = score
        top = jnp.max(score, axis=0, keepdims=True)
        chain(i, top_acc, jnp.maximum, [cut(top, p) for p in range(slots)])
        row_exp = jnp.exp(score - jnp.max(score, axis=1, keepdims=True))
        row_buf[i] = row_exp * (1.0 / jnp.sum(row_exp, axis=1, keepdims=True))

    @pl.loop(0, n_seq)
    def _(k):
        i = back(k)
        col_exp = jnp.exp(score_buf[i] - spread_out(i, top_acc))
        col_buf[i] = col_exp
        total = jnp.sum(col_exp, axis=0, keepdims=True)
        chain(i, sum_acc, add, [cut(total, p) for p in range(slots)])

    sum_acc[...] = 1.0 / sum_acc[...]

    @pl.loop(0, n_seq)
    def _(k):
        i = back(k)
        arrive_one(VALUE, k)
        chain(i, text_acc, add, blocks(tn(col_buf[i].astype(BF16), land[VALUE][i])))

    @pl.loop(0, n_seq)
    def _(k):
        j = back(k)
        at = newest[j]
        weight = jnp.transpose(jnp.broadcast_to(sum_acc[at], (blk, blk)))
        results[TEXT_OUT][j] = (text_acc[at] * weight).astype(BF16)

    arrive(TVAL)

    @pl.loop(0, n_seq)
    def _(k):
        i = back(k)
        pick(i, land[TVAL], t_sel)
        video_f = nn(row_buf[i].astype(BF16), t_sel[...])
        video_buf[i] = video_f
        results[VIDEO_OUT][i] = video_f.astype(BF16)

    send_all(TEXT_OUT, VIDEO_OUT)

    arrive(TCOT)

    @pl.loop(0, n_seq)
    def _(k):
        i = back(k)
        pick(i, land[TCOT], c_sel)
        col_exp = col_buf[i]
        col_prob = col_exp * spread_out(i, sum_acc)
        results[VALUE_GRAD][i] = nn(col_prob.astype(BF16), c_sel[...]).astype(BF16)
        col_dp = nt(land[VALUE][i], c_sel[...])
        dots = jnp.sum(col_exp * col_dp, axis=0, keepdims=True)
        chain(i, dot_acc, add, [cut(dots, p) for p in range(slots)])
        col_buf[i] = col_prob
        dot_buf[i] = col_dp

    dot_acc[...] = dot_acc[...] * sum_acc[...]
    send_all(VALUE_GRAD)


    @pl.loop(0, n_seq)
    def _(k):
        i = back(k)
        arrive_one(COT, k)
        chain(i, tval_acc, add, blocks(tn(row_buf[i].astype(BF16), land[COT][i])))

    @pl.loop(0, n_seq)
    def _(k):
        j = back(k)
        results[TVAL_GRAD][j] = tval_acc[newest[j]].astype(BF16)
        send_out(TVAL_GRAD, k)

    @pl.loop(0, n_seq)
    def _(k):
        i = back(k)
        pick(i, land[KEY], k_sel)
        pick(i, land[TVAL], t_sel)
        cot = land[COT][i]
        row_dp = nt(cot, t_sel[...])
        row_delta = jnp.sum(cot.astype(F32) * video_buf[i], axis=1, keepdims=True)
        grad = row_buf[i] * (row_dp - row_delta) + col_buf[i] * (dot_buf[i] - spread_out(i, dot_acc))
        tally = jnp.sum(grad * score_buf[i], axis=0, keepdims=True)
        for p in range(slots):
            scale_acc[...] += cut(tally, p)
        grad_half = (mult * grad).astype(BF16)
        results[QUERY_GRAD][i] = (nn(grad_half, k_sel[...]) * scale).astype(BF16)
        send_out(QUERY_GRAD, k)
        chain(i, key_acc, add, blocks(tn(grad_half, land[QUERY][i]) * scale))

    total = jnp.sum(scale_acc[...], axis=1, keepdims=True) / mult
    scale_own[...] = jnp.broadcast_to(total, scale_own.shape)

    @pl.loop(0, n_seq)
    def _(k):
        either(k + core == 0, lambda: scale_copy_own().start(), lambda: scale_copy(0, k).start())
        scale_copy(1, k).start()

    @pl.loop(0, n_seq)
    def _(k):
        j = back(k)
        results[KEY_GRAD][j] = key_acc[newest[j]].astype(BF16)
        send_out(KEY_GRAD, k)

    @pl.loop(0, n_seq)
    def _(k):
        either(k + core == 0, lambda: scale_copy_own().wait(), lambda: scale_copy(0, k).wait())
        scale_copy(1, k).wait()

    lane = lax.broadcasted_iota(jnp.int32, scale_out.shape, 1)
    sums = jnp.zeros(scale_out.shape, F32)
    for h in range(n_seq):
        sums = jnp.where(lane == h, scale_land[0, h] + scale_land[1, h], sums)
    scale_out[...] = sums

    for a in range(6):

        @pl.loop(0, n_seq)
        def _(k):
            either(stays(a, k), lambda: outbound_own(a).wait(), lambda: outbound(a, k).wait())


def deliver_kernel(n_seq, *refs):
    srcs, scale_src, dsts, scale_out, sems = refs[:6], refs[6], refs[7:13], refs[13], refs[14]
    copies = [pltpu.make_async_copy(s, t, sems.at[a]) for a, (s, t) in enumerate(zip(srcs, dsts))]
    for c in copies:
        c.start()
    scale_out[...] = scale_src[:1, :n_seq]
    for c in copies:
        c.wait()


def on_device(n_seq, n_section, *arrays):
    rows, pair_blocks, multiplier = arrays[:6], arrays[6], arrays[8]
    blk, width = rows[0].shape[2:]
    d = width // multiplier.shape[1]
    slots = pair_blocks.shape[3]
    vmem = pl.BlockSpec(memory_space=pltpu.VMEM)
    hbm = pl.BlockSpec(memory_space=pltpu.HBM)
    flat = jax.ShapeDtypeStruct((blk, width), BF16)
    places = n_seq * slots + 1
    dma = pltpu.SemaphoreType.DMA

    fused = pl.pallas_call(
        functools.partial(fused_kernel, n_seq, n_section, slots, d ** (-0.5)),
        out_shape=(flat,) * 6
        + (
            jax.ShapeDtypeStruct((8, 128), F32),
            jax.ShapeDtypeStruct((n_seq, 1, slots), jnp.int32),
        ),
        in_specs=[hbm] * 8,
        out_specs=(vmem,) * 7 + (hbm,),
        scratch_shapes=[pltpu.VMEM((n_seq, blk, d), BF16)] * 12
        + [pltpu.VMEM((8, 128), F32)]
        + [pltpu.VMEM((n_seq, blk, slots * blk), F32)] * 4
        + [pltpu.VMEM((slots * blk, d), BF16)] * 3
        + [pltpu.VMEM((places, blk, d), F32)] * 3
        + [pltpu.VMEM((places, 1, blk), F32)] * 3
        + [pltpu.VMEM((1, blk), F32)]
        + [
            pltpu.SMEM((n_seq, 1, slots), jnp.int32),
            pltpu.SMEM((n_seq,), jnp.int32),
            pltpu.SMEM((places,), jnp.int32),
            pltpu.SMEM((places,), jnp.int32),
        ]
        + [dma((6, n_seq)), dma((6, n_seq)), dma((6,))] * 2
        + [dma((n_seq,)), dma((n_seq,)), dma]
        + [dma((2, n_seq)), dma((2, n_seq)), dma, dma, dma]
        + [pltpu.VMEM((2, n_seq, 8, 128), F32)]
        + [pltpu.VMEM(multiplier.shape, F32), pltpu.SMEM(multiplier.shape, F32)]
        + [pltpu.VMEM((n_seq, blk, d), F32)],
        compiler_params=pltpu.CompilerParams(
            collective_id=0, has_side_effects=True, vmem_limit_bytes=101 * 512 * 1024
        ),
        name="fused",
    )(*[x[0, 0] for x in rows], pair_blocks[0, 0], multiplier)

    delivered = pl.pallas_call(
        functools.partial(deliver_kernel, n_seq),
        out_shape=(flat,) * 6 + (jax.ShapeDtypeStruct((1, n_seq), F32),),
        in_specs=[vmem] * 7,
        out_specs=(hbm,) * 6 + (vmem,),
        scratch_shapes=[dma((6,))],
        compiler_params=pltpu.CompilerParams(vmem_limit_bytes=2 * 1024 * 1024),
        name="deliver",
    )(*fused[:7])
    return tuple(x[None, None] for x in delivered[:6]) + (delivered[6],)


def solution(mesh):
    main = P("section", "dp", "seq", None)
    in_specs = (main,) * 7 + (P("section", "dp", "seq"), P("section", None))
    out_specs = (main,) * 6 + (P("section", None),)
    body = functools.partial(on_device, mesh.shape["seq"], mesh.shape["section"])
    return jax.shard_map(body, mesh=mesh, in_specs=in_specs, out_specs=out_specs, check_vma=False)
```

```python
import functools

import jax
import jax.numpy as jnp
from jax import lax
from jax.experimental import pallas as pl
from jax.experimental.pallas import tpu as pltpu
from jax.sharding import PartitionSpec as P

MESH = pl.DeviceIdType.MESH
NEG_FILL = -1e30
F32 = jnp.float32
BF16 = jnp.bfloat16
NT_DIMS = (((1,), (1,)), ((), ()))
TN_DIMS = (((0,), (0,)), ((), ()))
QUERY, VALUE, COT, KEY, TVAL, TCOT = range(6)
VIDEO_OUT, TEXT_OUT, QUERY_GRAD, VALUE_GRAD, KEY_GRAD, TVAL_GRAD = range(6)
ARRIVAL = (KEY, QUERY, VALUE, TVAL, TCOT, COT)


def fused_kernel(n_seq, n_section, slots, scale, *refs):
    srcs, pair_src, mult_src = refs[:6], refs[6], refs[7]
    outs, scale_out, pair_all = refs[8:14], refs[14], refs[15]
    land, results, scale_own = refs[16:22], refs[22:28], refs[28]
    score_buf, row_buf, col_buf, dot_buf = refs[29:33]
    k_sel, t_sel, c_sel = refs[33:36]
    text_acc, key_acc, tval_acc = refs[36:39]
    top_acc, sum_acc, dot_acc, scale_acc = refs[39:43]
    pairs, newest, prior, final = refs[43:47]
    (in_send, in_recv, in_own, out_send, out_recv, out_own, pair_send, pair_recv, pair_own) = refs[47:56]
    scale_send, scale_recv, mult_send, mult_recv, own_sem = refs[56:61]
    scale_land, mult_land, mult_ref, video_buf = refs[61:]

    me, section, core = lax.axis_index("seq"), lax.axis_index("section"), lax.axis_index("dp")
    before = lax.rem(section + n_section - 1, n_section)
    after = lax.rem(section + 1, n_section)
    worker = lax.rem(section + n_section - core, n_section)
    home = lax.rem(section + core, n_section)
    previous = lax.rem(section + core + n_section - 1, n_section)
    blk, d = land[0].shape[1:]
    wide = slots * blk
    empty = n_seq * slots
    mine = pl.ds(pl.multiple_of(me * d, d), d)

    def turn(k):
        return lax.rem(me + k * 9, n_seq)

    def back(k):
        return lax.rem(me + k * (n_seq - 9), n_seq)

    def nt(x, y):
        return lax.dot_general(x, y, NT_DIMS, preferred_element_type=F32)

    def tn(x, y):
        return lax.dot_general(x, y, TN_DIMS, preferred_element_type=F32)

    def nn(x, y):
        return jnp.dot(x, y, preferred_element_type=F32)

    def half(x):
        return x.astype(BF16).astype(F32)

    def remote(src, dst, send, recv, **where):
        return pltpu.make_async_remote_copy(
            src_ref=src, dst_ref=dst, send_sem=send, recv_sem=recv, device_id=where, device_id_type=MESH
        )

    def inbound(a, k):
        peer = turn(k)
        piece = srcs[a].at[:, pl.ds(pl.multiple_of(peer * d, d), d)]
        return remote(
            piece, land[a].at[me], in_send.at[a, k], in_recv.at[a, k], seq=peer, section=worker
        )

    def inbound_own(a):
        return pltpu.make_async_copy(srcs[a].at[:, mine], land[a].at[me], in_own.at[a])

    def pair_copy(k):
        return remote(
            pair_src, pair_all.at[me], pair_send.at[k], pair_recv.at[k], seq=turn(k), section=worker
        )

    def pair_copy_own():
        return pltpu.make_async_copy(pair_src, pair_all.at[me], pair_own)

    def outbound(a, k):
        peer = back(k)
        ends = (results[a].at[peer], outs[a].at[:, mine], out_send.at[a, k], out_recv.at[a, k])
        where = home if a in (VIDEO_OUT, TEXT_OUT) else previous
        return remote(*ends, seq=peer, section=where)

    def outbound_own(a):
        return pltpu.make_async_copy(results[a].at[me], outs[a].at[:, mine], out_own.at[a])

    def either(is_own, own, other):
        pl.when(is_own)(own)
        pl.when(jnp.logical_not(is_own))(other)

    def stays(a, k):
        return k + (core if a in (VIDEO_OUT, TEXT_OUT) else 1 - core) == 0

    def send_out(a, k):
        either(stays(a, k), lambda: outbound_own(a).start(), lambda: outbound(a, k).start())

    def send_all(*kinds):
        for a in kinds:

            @pl.loop(0, n_seq)
            def _(k):
                send_out(a, k)

    def scale_copy(other, k):
        return remote(
            scale_own,
            scale_land.at[core, me],
            scale_send.at[other, k],
            scale_recv.at[other, k],
            seq=turn(k),
            section=home,
            dp=(1 - core) if other else core,
        )

    def scale_copy_own():
        return pltpu.make_async_copy(scale_own, scale_land.at[core, me], own_sem)

    def mult_copy():
        return remote(mult_src, mult_land, mult_send, mult_recv, section=worker)

    def mult_copy_own():
        return pltpu.make_async_copy(mult_src, mult_land, own_sem)

    barrier = pltpu.get_barrier_semaphore()

    @pl.loop(1, n_seq)
    def _(k):
        pl.semaphore_signal(barrier, inc=1, device_id={"seq": turn(k)}, device_id_type=MESH)

    def signal_all(where, to):
        @pl.loop(0, n_seq)
        def _(k):
            there = {"seq": turn(k), "section": where, "dp": to}
            pl.semaphore_signal(barrier, inc=1, device_id=there, device_id_type=MESH)

    signal_all(after, core)

    @pl.when(core == 0)
    def _():
        signal_all(before, 1)
        pl.semaphore_wait(barrier, 3 * n_seq - 1)

    @pl.when(core == 1)
    def _():
        signal_all(before, 1)
        signal_all(section, 0)
        pl.semaphore_wait(barrier, 4 * n_seq - 1)

    @pl.loop(0, n_seq)
    def _(k):
        either(k + core == 0, lambda: pair_copy_own().start(), lambda: pair_copy(k).start())

    either(core == 0, lambda: mult_copy_own().start(), lambda: mult_copy().start())
    for a in ARRIVAL:

        @pl.loop(0, n_seq)
        def _(k):
            either(k + core == 0, lambda: inbound_own(a).start(), lambda: inbound(a, k).start())

    @pl.loop(0, n_seq)
    def _(k):
        either(k + core == 0, lambda: pair_copy_own().wait(), lambda: pair_copy(k).wait())

    either(core == 0, lambda: mult_copy_own().wait(), lambda: mult_copy().wait())
    fetch_mult = pltpu.make_async_copy(mult_land, mult_ref, own_sem)
    fetch_mult.start()
    fetch_mult.wait()
    mult = mult_ref[0, me]

    listed = pltpu.make_async_copy(pair_all, pairs, pair_own)
    listed.start()
    text_acc[empty] = jnp.zeros((blk, d), F32)
    key_acc[empty] = jnp.zeros((blk, d), F32)
    tval_acc[empty] = jnp.zeros((blk, d), F32)
    top_acc[empty] = jnp.full((1, blk), NEG_FILL, F32)
    sum_acc[empty] = jnp.zeros((1, blk), F32)
    dot_acc[empty] = jnp.zeros((1, blk), F32)
    scale_acc[...] = jnp.zeros_like(scale_acc)
    listed.wait()

    for j in range(n_seq):
        newest[j] = empty

    @pl.loop(0, n_seq)
    def _(k):
        i = back(k)
        for p in range(slots):
            j = pairs[i, 0, p]
            slot = i * slots + p
            prior[slot] = jnp.where(j >= 0, newest[jnp.maximum(j, 0)], empty)
            for b in range(n_seq):
                newest[b] = jnp.where(j == b, slot, newest[b])

    @pl.loop(0, n_seq)
    def _(i):
        for p in range(slots):
            final[i * slots + p] = newest[jnp.maximum(pairs[i, 0, p], 0)]

    def arrive_one(a, k):
        either(k + core == 0, lambda: inbound_own(a).wait(), lambda: inbound(a, k).wait())

    def arrive(a):
        @pl.loop(0, n_seq)
        def _(k):
            arrive_one(a, k)

    def cut(x, p):
        return x[:, p * blk : (p + 1) * blk]

    def pick(i, source, held):
        for p in range(slots):
            held[p * blk : (p + 1) * blk, :] = source[jnp.maximum(pairs[i, 0, p], 0)]

    def spread_out(i, rows):
        return jnp.concatenate([rows[final[i * slots + p]] for p in range(slots)], axis=1)

    def chain(i, acc, join, parts):
        for p in range(slots):
            slot = i * slots + p
            acc[slot] = join(acc[prior[slot]], parts[p])

    def add(x, y):
        return x + y

    def blocks(piece):
        return [half(piece[p * blk : (p + 1) * blk]) for p in range(slots)]

    arrive(KEY)

    @pl.loop(0, n_seq)
    def _(k):
        i = back(k)
        arrive_one(QUERY, k)
        pick(i, land[KEY], k_sel)
        score = nt(land[QUERY][i], k_sel[...]) * (mult * scale)
        score = jnp.concatenate(
            [
                jnp.where(pairs[i, 0, p] >= 0, cut(score, p), NEG_FILL)
                for p in range(slots)
            ],
            axis=1,
        )
        score_buf[i] = score
        top = jnp.max(score, axis=0, keepdims=True)
        chain(i, top_acc, jnp.maximum, [cut(top, p) for p in range(slots)])
        row_exp = jnp.exp(score - jnp.max(score, axis=1, keepdims=True))
        row_buf[i] = row_exp * (1.0 / jnp.sum(row_exp, axis=1, keepdims=True))

    @pl.loop(0, n_seq)
    def _(k):
        i = back(k)
        col_exp = jnp.exp(score_buf[i] - spread_out(i, top_acc))
        col_buf[i] = col_exp
        total = jnp.sum(col_exp, axis=0, keepdims=True)
        chain(i, sum_acc, add, [cut(total, p) for p in range(slots)])

    sum_acc[...] = 1.0 / sum_acc[...]

    @pl.loop(0, n_seq)
    def _(k):
        i = back(k)
        arrive_one(VALUE, k)
        chain(i, text_acc, add, blocks(tn(col_buf[i].astype(BF16), land[VALUE][i])))

    @pl.loop(0, n_seq)
    def _(k):
        j = back(k)
        at = newest[j]
        weight = jnp.transpose(jnp.broadcast_to(sum_acc[at], (blk, blk)))
        results[TEXT_OUT][j] = (text_acc[at] * weight).astype(BF16)

    arrive(TVAL)

    @pl.loop(0, n_seq)
    def _(k):
        i = back(k)
        pick(i, land[TVAL], t_sel)
        video_f = nn(row_buf[i].astype(BF16), t_sel[...])
        video_buf[i] = video_f
        results[VIDEO_OUT][i] = video_f.astype(BF16)

    send_all(VIDEO_OUT, TEXT_OUT)

    arrive(TCOT)

    @pl.loop(0, n_seq)
    def _(k):
        i = back(k)
        pick(i, land[TCOT], c_sel)
        col_exp = col_buf[i]
        col_prob = col_exp * spread_out(i, sum_acc)
        results[VALUE_GRAD][i] = nn(col_prob.astype(BF16), c_sel[...]).astype(BF16)
        col_dp = nt(land[VALUE][i], c_sel[...])
        dots = jnp.sum(col_exp * col_dp, axis=0, keepdims=True)
        chain(i, dot_acc, add, [cut(dots, p) for p in range(slots)])
        col_buf[i] = col_prob
        dot_buf[i] = col_dp

    dot_acc[...] = dot_acc[...] * sum_acc[...]
    send_all(VALUE_GRAD)


    @pl.loop(0, n_seq)
    def _(k):
        i = back(k)
        arrive_one(COT, k)
        chain(i, tval_acc, add, blocks(tn(row_buf[i].astype(BF16), land[COT][i])))

    @pl.loop(0, n_seq)
    def _(k):
        j = back(k)
        results[TVAL_GRAD][j] = tval_acc[newest[j]].astype(BF16)
        send_out(TVAL_GRAD, k)

    @pl.loop(0, n_seq)
    def _(k):
        i = back(k)
        pick(i, land[KEY], k_sel)
        pick(i, land[TVAL], t_sel)
        cot = land[COT][i]
        row_dp = nt(cot, t_sel[...])
        row_delta = jnp.sum(cot.astype(F32) * video_buf[i], axis=1, keepdims=True)
        grad = row_buf[i] * (row_dp - row_delta) + col_buf[i] * (dot_buf[i] - spread_out(i, dot_acc))
        tally = jnp.sum(grad * score_buf[i], axis=0, keepdims=True)
        for p in range(slots):
            scale_acc[...] += cut(tally, p)
        grad_half = (mult * grad).astype(BF16)
        results[QUERY_GRAD][i] = (nn(grad_half, k_sel[...]) * scale).astype(BF16)
        send_out(QUERY_GRAD, k)
        chain(i, key_acc, add, blocks(tn(grad_half, land[QUERY][i]) * scale))

    total = jnp.sum(scale_acc[...], axis=1, keepdims=True) / mult
    scale_own[...] = jnp.broadcast_to(total, scale_own.shape)

    @pl.loop(0, n_seq)
    def _(k):
        either(k + core == 0, lambda: scale_copy_own().start(), lambda: scale_copy(0, k).start())
        scale_copy(1, k).start()

    @pl.loop(0, n_seq)
    def _(k):
        j = back(k)
        results[KEY_GRAD][j] = key_acc[newest[j]].astype(BF16)
        send_out(KEY_GRAD, k)

    @pl.loop(0, n_seq)
    def _(k):
        either(k + core == 0, lambda: scale_copy_own().wait(), lambda: scale_copy(0, k).wait())
        scale_copy(1, k).wait()

    lane = lax.broadcasted_iota(jnp.int32, scale_out.shape, 1)
    sums = jnp.zeros(scale_out.shape, F32)
    for h in range(n_seq):
        sums = jnp.where(lane == h, scale_land[0, h] + scale_land[1, h], sums)
    scale_out[...] = sums

    for a in (VIDEO_OUT, TEXT_OUT, VALUE_GRAD, TVAL_GRAD, QUERY_GRAD, KEY_GRAD):

        @pl.loop(0, n_seq)
        def _(k):
            either(stays(a, k), lambda: outbound_own(a).wait(), lambda: outbound(a, k).wait())


def deliver_kernel(n_seq, *refs):
    srcs, scale_src, dsts, scale_out, sems = refs[:6], refs[6], refs[7:13], refs[13], refs[14]
    copies = [pltpu.make_async_copy(s, t, sems.at[a]) for a, (s, t) in enumerate(zip(srcs, dsts))]
    for c in copies:
        c.start()
    scale_out[...] = scale_src[:, :n_seq]
    for c in copies:
        c.wait()


def on_device(n_seq, n_section, *arrays):
    rows, pair_blocks, multiplier = arrays[:6], arrays[6], arrays[8]
    blk, width = rows[0].shape[2:]
    d = width // multiplier.shape[1]
    slots = pair_blocks.shape[3]
    vmem = pl.BlockSpec(memory_space=pltpu.VMEM)
    hbm = pl.BlockSpec(memory_space=pltpu.HBM)
    flat = jax.ShapeDtypeStruct((blk, width), BF16)
    places = n_seq * slots + 1
    dma = pltpu.SemaphoreType.DMA

    fused = pl.pallas_call(
        functools.partial(fused_kernel, n_seq, n_section, slots, d ** (-0.5)),
        out_shape=(flat,) * 6
        + (
            jax.ShapeDtypeStruct((1, 128), F32),
            jax.ShapeDtypeStruct((n_seq, 1, slots), jnp.int32),
        ),
        in_specs=[hbm] * 8,
        out_specs=(vmem,) * 7 + (hbm,),
        scratch_shapes=[pltpu.VMEM((n_seq, blk, d), BF16)] * 12
        + [pltpu.VMEM((1, 128), F32)]
        + [pltpu.VMEM((n_seq, blk, slots * blk), F32)] * 4
        + [pltpu.VMEM((slots * blk, d), BF16)] * 3
        + [pltpu.VMEM((places, blk, d), F32)] * 3
        + [pltpu.VMEM((places, 1, blk), F32)] * 3
        + [pltpu.VMEM((1, blk), F32)]
        + [
            pltpu.SMEM((n_seq, 1, slots), jnp.int32),
            pltpu.SMEM((n_seq,), jnp.int32),
            pltpu.SMEM((places,), jnp.int32),
            pltpu.SMEM((places,), jnp.int32),
        ]
        + [dma((6, n_seq)), dma((6, n_seq)), dma((6,))] * 2
        + [dma((n_seq,)), dma((n_seq,)), dma]
        + [dma((2, n_seq)), dma((2, n_seq)), dma, dma, dma]
        + [pltpu.VMEM((2, n_seq, 1, 128), F32)]
        + [pltpu.VMEM(multiplier.shape, F32), pltpu.SMEM(multiplier.shape, F32)]
        + [pltpu.VMEM((n_seq, blk, d), F32)],
        compiler_params=pltpu.CompilerParams(
            collective_id=0, has_side_effects=True, vmem_limit_bytes=101 * 512 * 1024
        ),
        name="fused",
    )(*[x[0, 0] for x in rows], pair_blocks[0, 0], multiplier)

    delivered = pl.pallas_call(
        functools.partial(deliver_kernel, n_seq),
        out_shape=(flat,) * 6 + (jax.ShapeDtypeStruct((1, n_seq), F32),),
        in_specs=[vmem] * 7,
        out_specs=(hbm,) * 6 + (vmem,),
        scratch_shapes=[dma((6,))],
        compiler_params=pltpu.CompilerParams(vmem_limit_bytes=2 * 1024 * 1024),
        name="deliver",
    )(*fused[:7])
    return tuple(x[None, None] for x in delivered[:6]) + (delivered[6],)


def solution(mesh):
    main = P("section", "dp", "seq", None)
    in_specs = (main,) * 7 + (P("section", "dp", "seq"), P("section", None))
    out_specs = (main,) * 6 + (P("section", None),)
    body = functools.partial(on_device, mesh.shape["seq"], mesh.shape["section"])
    return jax.shard_map(body, mesh=mesh, in_specs=in_specs, out_specs=out_specs, check_vma=False)
```

```python
import functools

import jax
import jax.numpy as jnp
from jax import lax
from jax.experimental import pallas as pl
from jax.experimental.pallas import tpu as pltpu
from jax.sharding import PartitionSpec as P

MESH = pl.DeviceIdType.MESH
NEG_FILL = -1e30
F32 = jnp.float32
BF16 = jnp.bfloat16
NT_DIMS = (((1,), (1,)), ((), ()))
TN_DIMS = (((0,), (0,)), ((), ()))
QUERY, VALUE, COT, KEY, TVAL, TCOT = range(6)
VIDEO_OUT, TEXT_OUT, QUERY_GRAD, VALUE_GRAD, KEY_GRAD, TVAL_GRAD = range(6)
ARRIVAL = (KEY, QUERY, VALUE, TVAL, TCOT, COT)


def fused_kernel(n_seq, n_section, slots, scale, *refs):
    srcs, pair_src, mult_src = refs[:6], refs[6], refs[7]
    outs, scale_out, pair_all = refs[8:14], refs[14], refs[15]
    land, results, scale_own = refs[16:22], refs[22:28], refs[28]
    score_buf, row_buf, col_buf, dot_buf = refs[29:33]
    k_sel, t_sel, c_sel = refs[33:36]
    text_acc, key_acc, tval_acc = refs[36:39]
    top_acc, sum_acc, dot_acc, scale_acc = refs[39:43]
    pairs, newest, prior, final = refs[43:47]
    (in_send, in_recv, in_own, out_send, out_recv, out_own, pair_send, pair_recv, pair_own) = refs[47:56]
    scale_send, scale_recv, mult_send, mult_recv, own_sem = refs[56:61]
    scale_land, mult_land, mult_ref, video_buf = refs[61:]

    me, section, core = lax.axis_index("seq"), lax.axis_index("section"), lax.axis_index("dp")
    before = lax.rem(section + n_section - 1, n_section)
    after = lax.rem(section + 1, n_section)
    worker = lax.rem(section + n_section - core, n_section)
    home = lax.rem(section + core, n_section)
    previous = lax.rem(section + core + n_section - 1, n_section)
    blk, d = land[0].shape[1:]
    wide = slots * blk
    empty = n_seq * slots
    mine = pl.ds(pl.multiple_of(me * d, d), d)

    def turn(k):
        return lax.rem(me + k * 9, n_seq)

    def back(k):
        return lax.rem(me + k * (n_seq - 9), n_seq)

    def nt(x, y):
        return lax.dot_general(x, y, NT_DIMS, preferred_element_type=F32)

    def tn(x, y):
        return lax.dot_general(x, y, TN_DIMS, preferred_element_type=F32)

    def nn(x, y):
        return jnp.dot(x, y, preferred_element_type=F32)

    def half(x):
        return x.astype(BF16).astype(F32)

    def remote(src, dst, send, recv, **where):
        return pltpu.make_async_remote_copy(
            src_ref=src, dst_ref=dst, send_sem=send, recv_sem=recv, device_id=where, device_id_type=MESH
        )

    def inbound(a, k):
        peer = turn(k)
        piece = srcs[a].at[:, pl.ds(pl.multiple_of(peer * d, d), d)]
        return remote(
            piece, land[a].at[me], in_send.at[a, k], in_recv.at[a, k], seq=peer, section=worker
        )

    def inbound_own(a):
        return pltpu.make_async_copy(srcs[a].at[:, mine], land[a].at[me], in_own.at[a])

    def pair_copy(k):
        return remote(
            pair_src, pair_all.at[me], pair_send.at[k], pair_recv.at[k], seq=turn(k), section=worker
        )

    def pair_copy_own():
        return pltpu.make_async_copy(pair_src, pair_all.at[me], pair_own)

    def outbound(a, k):
        peer = back(k)
        ends = (results[a].at[peer], outs[a].at[:, mine], out_send.at[a, k], out_recv.at[a, k])
        where = home if a in (VIDEO_OUT, TEXT_OUT) else previous
        return remote(*ends, seq=peer, section=where)

    def outbound_own(a):
        return pltpu.make_async_copy(results[a].at[me], outs[a].at[:, mine], out_own.at[a])

    def either(is_own, own, other):
        pl.when(is_own)(own)
        pl.when(jnp.logical_not(is_own))(other)

    def stays(a, k):
        return k + (core if a in (VIDEO_OUT, TEXT_OUT) else 1 - core) == 0

    def send_out(a, k):
        either(stays(a, k), lambda: outbound_own(a).start(), lambda: outbound(a, k).start())

    def send_all(*kinds):
        for a in kinds:

            @pl.loop(0, n_seq)
            def _(k):
                send_out(a, k)

    def scale_copy(other, k):
        return remote(
            scale_own,
            scale_land.at[core, me],
            scale_send.at[other, k],
            scale_recv.at[other, k],
            seq=turn(k),
            section=home,
            dp=(1 - core) if other else core,
        )

    def scale_copy_own():
        return pltpu.make_async_copy(scale_own, scale_land.at[core, me], own_sem)

    def mult_copy():
        return remote(mult_src, mult_land, mult_send, mult_recv, section=worker)

    def mult_copy_own():
        return pltpu.make_async_copy(mult_src, mult_land, own_sem)

    barrier = pltpu.get_barrier_semaphore()

    @pl.loop(1, n_seq)
    def _(k):
        pl.semaphore_signal(barrier, inc=1, device_id={"seq": turn(k)}, device_id_type=MESH)

    def signal_all(where, to):
        @pl.loop(0, n_seq)
        def _(k):
            there = {"seq": turn(k), "section": where, "dp": to}
            pl.semaphore_signal(barrier, inc=1, device_id=there, device_id_type=MESH)

    signal_all(after, core)

    @pl.when(core == 0)
    def _():
        signal_all(before, 1)
        pl.semaphore_wait(barrier, 3 * n_seq - 1)

    @pl.when(core == 1)
    def _():
        signal_all(before, 1)
        signal_all(section, 0)
        pl.semaphore_wait(barrier, 4 * n_seq - 1)

    @pl.loop(0, n_seq)
    def _(k):
        either(k + core == 0, lambda: pair_copy_own().start(), lambda: pair_copy(k).start())

    either(core == 0, lambda: mult_copy_own().start(), lambda: mult_copy().start())
    for a in ARRIVAL:

        @pl.loop(0, n_seq)
        def _(k):
            either(k + core == 0, lambda: inbound_own(a).start(), lambda: inbound(a, k).start())

    @pl.loop(0, n_seq)
    def _(k):
        either(k + core == 0, lambda: pair_copy_own().wait(), lambda: pair_copy(k).wait())

    either(core == 0, lambda: mult_copy_own().wait(), lambda: mult_copy().wait())
    fetch_mult = pltpu.make_async_copy(mult_land, mult_ref, own_sem)
    fetch_mult.start()
    fetch_mult.wait()
    mult = mult_ref[0, me]

    listed = pltpu.make_async_copy(pair_all, pairs, pair_own)
    listed.start()
    text_acc[empty] = jnp.zeros((blk, d), F32)
    key_acc[empty] = jnp.zeros((blk, d), F32)
    tval_acc[empty] = jnp.zeros((blk, d), F32)
    top_acc[empty] = jnp.full((1, blk), NEG_FILL, F32)
    sum_acc[empty] = jnp.zeros((1, blk), F32)
    dot_acc[empty] = jnp.zeros((1, blk), F32)
    scale_acc[...] = jnp.zeros_like(scale_acc)
    listed.wait()

    for j in range(n_seq):
        newest[j] = empty

    @pl.loop(0, n_seq)
    def _(k):
        i = back(k)
        for p in range(slots):
            j = pairs[i, 0, p]
            slot = i * slots + p
            prior[slot] = jnp.where(j >= 0, newest[jnp.maximum(j, 0)], empty)
            for b in range(n_seq):
                newest[b] = jnp.where(j == b, slot, newest[b])

    @pl.loop(0, n_seq)
    def _(i):
        for p in range(slots):
            final[i * slots + p] = newest[jnp.maximum(pairs[i, 0, p], 0)]

    def arrive_one(a, k):
        either(k + core == 0, lambda: inbound_own(a).wait(), lambda: inbound(a, k).wait())

    def arrive(a):
        @pl.loop(0, n_seq)
        def _(k):
            arrive_one(a, k)

    def cut(x, p):
        return x[:, p * blk : (p + 1) * blk]

    def pick(i, source, held):
        for p in range(slots):
            held[p * blk : (p + 1) * blk, :] = source[jnp.maximum(pairs[i, 0, p], 0)]

    def spread_out(i, rows):
        return jnp.concatenate([rows[final[i * slots + p]] for p in range(slots)], axis=1)

    def chain(i, acc, join, parts):
        for p in range(slots):
            slot = i * slots + p
            acc[slot] = join(acc[prior[slot]], parts[p])

    def add(x, y):
        return x + y

    def blocks(piece):
        return [half(piece[p * blk : (p + 1) * blk]) for p in range(slots)]

    arrive(KEY)

    @pl.loop(0, n_seq)
    def _(k):
        i = back(k)
        arrive_one(QUERY, k)
        pick(i, land[KEY], k_sel)
        score = nt(land[QUERY][i], k_sel[...]) * (mult * scale)
        score = jnp.concatenate(
            [
                jnp.where(pairs[i, 0, p] >= 0, cut(score, p), NEG_FILL)
                for p in range(slots)
            ],
            axis=1,
        )
        score_buf[i] = score
        top = jnp.max(score, axis=0, keepdims=True)
        chain(i, top_acc, jnp.maximum, [cut(top, p) for p in range(slots)])
        row_exp = jnp.exp(score - jnp.max(score, axis=1, keepdims=True))
        row_buf[i] = row_exp * (1.0 / jnp.sum(row_exp, axis=1, keepdims=True))

    @pl.loop(0, n_seq)
    def _(k):
        i = back(k)
        col_exp = jnp.exp(score_buf[i] - spread_out(i, top_acc))
        col_buf[i] = col_exp
        total = jnp.sum(col_exp, axis=0, keepdims=True)
        chain(i, sum_acc, add, [cut(total, p) for p in range(slots)])

    sum_acc[...] = 1.0 / sum_acc[...]

    @pl.loop(0, n_seq)
    def _(k):
        i = back(k)
        arrive_one(VALUE, k)
        chain(i, text_acc, add, blocks(tn(col_buf[i].astype(BF16), land[VALUE][i])))

    @pl.loop(0, n_seq)
    def _(k):
        j = back(k)
        at = newest[j]
        weight = jnp.transpose(jnp.broadcast_to(sum_acc[at], (blk, blk)))
        results[TEXT_OUT][j] = (text_acc[at] * weight).astype(BF16)

    arrive(TVAL)

    @pl.loop(0, n_seq)
    def _(k):
        i = back(k)
        pick(i, land[TVAL], t_sel)
        video_f = nn(row_buf[i].astype(BF16), t_sel[...])
        video_buf[i] = video_f
        results[VIDEO_OUT][i] = video_f.astype(BF16)

    send_all(VIDEO_OUT, TEXT_OUT)

    arrive(TCOT)

    @pl.loop(0, n_seq)
    def _(k):
        i = back(k)
        pick(i, land[TCOT], c_sel)
        col_exp = col_buf[i]
        col_prob = col_exp * spread_out(i, sum_acc)
        results[VALUE_GRAD][i] = nn(col_prob.astype(BF16), c_sel[...]).astype(BF16)
        col_dp = nt(land[VALUE][i], c_sel[...])
        dots = jnp.sum(col_exp * col_dp, axis=0, keepdims=True)
        chain(i, dot_acc, add, [cut(dots, p) for p in range(slots)])
        col_buf[i] = col_prob
        dot_buf[i] = col_dp

    dot_acc[...] = dot_acc[...] * sum_acc[...]
    send_all(VALUE_GRAD)


    @pl.loop(0, n_seq)
    def _(k):
        i = back(k)
        arrive_one(COT, k)
        chain(i, tval_acc, add, blocks(tn(row_buf[i].astype(BF16), land[COT][i])))

    @pl.loop(0, n_seq)
    def _(k):
        j = back(k)
        results[TVAL_GRAD][j] = tval_acc[newest[j]].astype(BF16)
        send_out(TVAL_GRAD, k)

    @pl.loop(0, n_seq)
    def _(k):
        i = back(k)
        pick(i, land[KEY], k_sel)
        pick(i, land[TVAL], t_sel)
        cot = land[COT][i]
        row_dp = nt(cot, t_sel[...])
        row_delta = jnp.sum(cot.astype(F32) * video_buf[i], axis=1, keepdims=True)
        grad = row_buf[i] * (row_dp - row_delta) + col_buf[i] * (dot_buf[i] - spread_out(i, dot_acc))
        tally = jnp.sum(grad * score_buf[i], axis=0, keepdims=True)
        for p in range(slots):
            scale_acc[...] += cut(tally, p)
        grad_half = (mult * grad).astype(BF16)
        results[QUERY_GRAD][i] = (nn(grad_half, k_sel[...]) * scale).astype(BF16)
        send_out(QUERY_GRAD, k)
        chain(i, key_acc, add, blocks(tn(grad_half, land[QUERY][i]) * scale))

    total = jnp.sum(scale_acc[...], axis=1, keepdims=True) / mult
    scale_own[...] = jnp.broadcast_to(total, scale_own.shape)

    @pl.loop(0, n_seq)
    def _(k):
        either(k + core == 0, lambda: scale_copy_own().start(), lambda: scale_copy(0, k).start())
        scale_copy(1, k).start()

    @pl.loop(0, n_seq)
    def _(k):
        j = back(k)
        results[KEY_GRAD][j] = key_acc[newest[j]].astype(BF16)
        send_out(KEY_GRAD, k)

    @pl.loop(0, n_seq)
    def _(k):
        either(k + core == 0, lambda: scale_copy_own().wait(), lambda: scale_copy(0, k).wait())
        scale_copy(1, k).wait()

    lane = lax.broadcasted_iota(jnp.int32, scale_out.shape, 1)
    sums = jnp.zeros(scale_out.shape, F32)
    for h in range(n_seq):
        sums = jnp.where(lane == h, scale_land[0, h] + scale_land[1, h], sums)
    scale_out[...] = sums

    for a in (VIDEO_OUT, TEXT_OUT, VALUE_GRAD, TVAL_GRAD, QUERY_GRAD, KEY_GRAD):

        @pl.loop(0, n_seq)
        def _(k):
            either(stays(a, k), lambda: outbound_own(a).wait(), lambda: outbound(a, k).wait())


def deliver_kernel(n_seq, *refs):
    srcs, scale_src, dsts, scale_out, sems = refs[:6], refs[6], refs[7:13], refs[13], refs[14]
    copies = [pltpu.make_async_copy(s, t, sems.at[a]) for a, (s, t) in enumerate(zip(srcs, dsts))]
    for c in copies:
        c.start()
    scale_out[...] = scale_src[:, :n_seq]
    for c in copies:
        c.wait()


def on_device(n_seq, n_section, *arrays):
    rows, pair_blocks, multiplier = arrays[:6], arrays[6], arrays[8]
    blk, width = rows[0].shape[2:]
    d = width // multiplier.shape[1]
    slots = pair_blocks.shape[3]
    vmem = pl.BlockSpec(memory_space=pltpu.VMEM)
    hbm = pl.BlockSpec(memory_space=pltpu.HBM)
    flat = jax.ShapeDtypeStruct((blk, width), BF16)
    places = n_seq * slots + 1
    dma = pltpu.SemaphoreType.DMA

    fused = pl.pallas_call(
        functools.partial(fused_kernel, n_seq, n_section, slots, d ** (-0.5)),
        out_shape=(flat,) * 6
        + (
            jax.ShapeDtypeStruct((1, 128), F32),
            jax.ShapeDtypeStruct((n_seq, 1, slots), jnp.int32),
        ),
        in_specs=[hbm] * 8,
        out_specs=(vmem,) * 7 + (hbm,),
        scratch_shapes=[pltpu.VMEM((n_seq, blk, d), BF16)] * 12
        + [pltpu.VMEM((1, 128), F32)]
        + [pltpu.VMEM((n_seq, blk, slots * blk), F32)] * 4
        + [pltpu.VMEM((slots * blk, d), BF16)] * 3
        + [pltpu.VMEM((places, blk, d), F32)] * 3
        + [pltpu.VMEM((places, 1, blk), F32)] * 3
        + [pltpu.VMEM((1, blk), F32)]
        + [
            pltpu.SMEM((n_seq, 1, slots), jnp.int32),
            pltpu.SMEM((n_seq,), jnp.int32),
            pltpu.SMEM((places,), jnp.int32),
            pltpu.SMEM((places,), jnp.int32),
        ]
        + [dma((6, n_seq)), dma((6, n_seq)), dma((6,))] * 2
        + [dma((n_seq,)), dma((n_seq,)), dma]
        + [dma((2, n_seq)), dma((2, n_seq)), dma, dma, dma]
        + [pltpu.VMEM((2, n_seq, 1, 128), F32)]
        + [pltpu.VMEM(multiplier.shape, F32), pltpu.SMEM(multiplier.shape, F32)]
        + [pltpu.VMEM((n_seq, blk, d), F32)],
        compiler_params=pltpu.CompilerParams(
            collective_id=0, has_side_effects=True, vmem_limit_bytes=101 * 512 * 1024
        ),
        name="fused",
    )(*[x[0, 0] for x in rows], pair_blocks[0, 0], multiplier)

    delivered = pl.pallas_call(
        functools.partial(deliver_kernel, n_seq),
        out_shape=(flat,) * 6 + (jax.ShapeDtypeStruct((1, n_seq), F32),),
        in_specs=[vmem] * 7,
        out_specs=(hbm,) * 6 + (vmem,),
        scratch_shapes=[dma((6,))],
        compiler_params=pltpu.CompilerParams(vmem_limit_bytes=8 * 1024 * 1024),
        name="deliver",
    )(*fused[:7])
    return tuple(x[None, None] for x in delivered[:6]) + (delivered[6],)


def solution(mesh):
    main = P("section", "dp", "seq", None)
    in_specs = (main,) * 7 + (P("section", "dp", "seq"), P("section", None))
    out_specs = (main,) * 6 + (P("section", None),)
    body = functools.partial(on_device, mesh.shape["seq"], mesh.shape["section"])
    return jax.shard_map(body, mesh=mesh, in_specs=in_specs, out_specs=out_specs, check_vma=False)
```
